32 devices in a mesh: aux: 4 (over z), orb: 8 (over y, x, core).
Axes of the slice: x: 2, y: 2, z: 4, core: 2. Of those that a mesh axis runs over, the one named last changes fastest.
Arguments:
- integrals: bfloat16 [8, 1024, 1024], P('aux', 'orb'), may hold values from -0.1875 to 0.1875
- int_mask: int32 [4, 8, 8], P('aux', 'orb'), may hold values 0 or 1
- panels: bfloat16 [1024, 1024], P(None, 'orb'), may hold values from -6 to 6
- coef_mask: int32 [8, 8], replicated, may hold values 0 or 1
- owner_map: int32 [8], replicated, may hold values from 0 to 7, each once
Outputs:
- exchange: float32 [1024, 1024], P('orb', 'aux')
The draws below stay inside these ranges and needn't reach their ends.
Inputs may be any that keep to these rules, and one draw needn't show every extreme that they name: owner_map is a permutation of the orbital blocks.
All inputs are finite; a program needn't handle non-finite values. No bound on the sum of `int_mask` on one device may be relied on, other than what follows from the above.
Results may differ from the reference program's by a relative error of at most 0.0014.
Values may be sent and summed in bfloat16 or wider, within the bound.
A program may use at most 64 MiB of HBM per device.

```python
import jax
import jax.numpy as jnp
from jax import lax

BLK = 128
AUX_DEV = 2
NBAS = 1024
OBLK = 8
NOCC = 1024
AUXW = 8
N_AUX = 4
N_ORB = 8


def touch_ends(array, key, low, top_value):
    spot = [jax.random.randint(jax.random.fold_in(key, axis), (), 0, length) for axis, length in enumerate(array.shape)]
    widest = array.shape.index(max(array.shape))
    beside = spot[:widest] + [(spot[widest] + 1) % array.shape[widest]] + spot[widest + 1:]
    return array.at[tuple(spot)].set(low).at[tuple(beside)].set(top_value)


def shard_levels(own_key, dims, split, smallest, top_value):
    level, own = 1.0, jax.random.fold_in(own_key, 6)
    for dim, parts in split:
        draws = jnp.exp(jax.random.uniform(jax.random.fold_in(own, dim), (parts,), jnp.float32, smallest / len(split), top_value / len(split)))
        level = level * jnp.repeat(draws, dims[dim] // parts).reshape([-1 if axis == dim else 1 for axis in range(len(dims))])
    return level


def normal_values(own_key, extent, deviation, most, cuts=(), kind=jnp.bfloat16):
    drawn = deviation * jax.random.normal(own_key, extent, jnp.float32)
    if cuts:
        drawn = drawn * shard_levels(own_key, extent, cuts, -0.22, 0.18)
    return jnp.clip(drawn, -most, most).astype(kind)


def setup_inputs(seed: int = 0) -> dict:
    streams_of = jax.random.split(jax.random.key(seed), 6)
    integrals = normal_values(streams_of[0], (AUXW, NBAS, NBAS), NBAS ** -0.5, 0.1875, ((0, 4), (1, 8)))
    int_mask = touch_ends((jax.random.randint(streams_of[1], (N_AUX, N_ORB, N_ORB), 0, 4) < 3).astype(jnp.int32), jax.random.fold_in(streams_of[1], 1), 0, 1)
    panels = normal_values(streams_of[2], (NBAS, NOCC), 1.0, 6.0, ((1, 8),))
    coef_mask = touch_ends((jax.random.randint(streams_of[3], (N_ORB, OBLK), 0, 4) < 3).astype(jnp.int32), jax.random.fold_in(streams_of[3], 1), 0, 1)
    owner_map = jax.random.permutation(streams_of[4], OBLK).astype(jnp.int32)
    return dict(integrals=integrals, int_mask=int_mask, panels=panels, coef_mask=coef_mask, owner_map=owner_map)


def reference(integrals, int_mask, panels, coef_mask, owner_map):
    block_mask = int_mask.astype(jnp.bfloat16)
    shaped = integrals.reshape(N_AUX, AUX_DEV, N_ORB, BLK, N_ORB, BLK)
    kept = shaped * block_mask[:, None, :, None, :, None]
    kept = kept.reshape(AUXW, NBAS, NBAS)
    blocks = panels.reshape(NBAS, OBLK, BLK)
    coef = jnp.take(blocks, owner_map, axis=1)
    coef = coef.reshape(N_ORB, BLK, OBLK, BLK) * coef_mask.astype(jnp.bfloat16)[:, None, :, None]
    coef = coef.reshape(NBAS, NOCC)

    def transform(slab):
        return jnp.dot(slab, coef, preferred_element_type=jnp.float32).astype(jnp.bfloat16)
    half = lax.map(transform, kept)

    def accumulate(total, slab):
        return (total + jnp.dot(slab, slab.T, preferred_element_type=jnp.float32), None)
    total, unused = lax.scan(accumulate, jnp.zeros((NBAS, NBAS), jnp.float32), half)
    return total / jnp.sqrt(jnp.float32(AUXW * NOCC))
```

```python
import functools

import jax
import jax.numpy as jnp
from jax import lax
from jax.experimental import pallas as pl
from jax.experimental.pallas import tpu as pltpu
from jax.sharding import PartitionSpec as P

NT = (((1,), (1,)), ((), ()))


def tile_product(mine, other):
    return jnp.einsum("pmi,pni->mn", mine, other, preferred_element_type=jnp.float32)


def local_collectives(integrals, int_mask, panels, coef_mask, owner_map):
    aux_local, rows, nbas = integrals.shape
    nblocks = int_mask.shape[2]
    width = nbas // nblocks
    keep = int_mask[0, 0].astype(jnp.bfloat16)
    kept = (integrals.reshape(aux_local, rows, nblocks, width) * keep[None, None, :, None]).reshape(
        aux_local, rows, nbas
    )
    gathered = lax.all_gather(panels, "orb", axis=1, tiled=True)
    nocc = gathered.shape[1]
    oblocks = nocc // width
    here = (owner_map[:, None] == jnp.arange(oblocks)[None, :]).astype(jnp.bfloat16)
    slot_mask = jnp.dot(coef_mask.astype(jnp.bfloat16), here)
    coef = gathered.reshape(nblocks, width, oblocks, width) * slot_mask[:, None, :, None]
    coef = coef.reshape(nbas, nocc)
    half = jnp.dot(kept.reshape(aux_local * rows, nbas), coef, preferred_element_type=jnp.float32)
    half = half.astype(jnp.bfloat16).reshape(aux_local, rows, nocc)
    partial_rows = tile_product(half, lax.all_gather(half, "orb", axis=1, tiled=True))
    scale_factor = 1.0 / jnp.sqrt(jnp.float32(aux_local * lax.axis_size("aux") * nocc))
    return lax.psum_scatter(partial_rows * scale_factor, "aux", scatter_dimension=1, tiled=True)


def kernel(
    scale, int_hbm, imask_hbm, pan_hbm, cmask_hbm, owner_hbm, out_ref,
    int_ref, imask_ref, pan_ref, cmask_ref, owner_ref,
    pan, kept, tacc, t2, part, zrecv, part16, insem, ssem, rsem, zsend, zsem, psend, psem,
):
    loads = [
        pltpu.make_async_copy(src, dst, insem.at[n])
        for n, (src, dst) in enumerate((
            (imask_hbm, imask_ref), (cmask_hbm, cmask_ref), (owner_hbm, owner_ref),
            (pan_hbm, pan_ref), (int_hbm, int_ref),
        ))
    ]
    for load in loads:
        load.start()
    me = lax.axis_index("orb")
    z = lax.axis_index("aux")
    core = lax.rem(me, 2)
    x = lax.rem(me // 2, 2)
    y = me // 4
    partner = me + 1 - 2 * core
    xn = me + 2 - 4 * x
    yn = me + 4 - 8 * y
    dn = xn + 4 - 8 * y
    chip, xchip, ychip, dchip = me // 2, xn // 2, yn // 2, dn // 2
    nz = 4
    aux_local, rows, nbas = int_ref.shape
    width = pan_ref.shape[1]
    nblocks = nbas // width
    q = rows // 4
    plane = 640
    share = (nbas - plane) // nz

    barrier = pltpu.get_barrier_semaphore()
    for other in (partner, xn, yn):
        pl.semaphore_signal(
            barrier, inc=1, device_id=(z, other), device_id_type=pl.DeviceIdType.MESH
        )
    for step in range(1, nz):
        pl.semaphore_signal(
            barrier, inc=1, device_id=(lax.rem(z + step, nz), me), device_id_type=pl.DeviceIdType.MESH
        )
    for load in loads[:4]:
        load.wait()

    block = jnp.int32(0)
    for j in range(nblocks):
        block = jnp.where(owner_ref[j] == me, j, block)
    for l in range(nblocks):
        cm = cmask_ref[l, block].astype(jnp.float32)
        sl = slice(l * width, (l + 1) * width)
        pan[me, sl, :] = (pan_ref[sl, :].astype(jnp.float32) * cm).astype(jnp.bfloat16)

    pl.semaphore_wait(barrier, 3 + nz - 1)

    pending = []

    def copy(kind, ref, dev):
        return pltpu.make_async_remote_copy(
            src_ref=ref, dst_ref=ref, send_sem=ssem.at[kind], recv_sem=rsem.at[kind],
            device_id=(z, dev), device_id_type=pl.DeviceIdType.MESH,
        )

    def send(kind, ref, dev):
        c = copy(kind, ref, dev)
        c.start()
        pending.append(c)

    def recv(kind, ref, dev):
        copy(kind, ref, dev).wait_recv()

    def inhalf(slot, h):
        return pan.at[slot, pl.ds(h * plane // 2, plane // 2)]

    def shared(slot, src):
        return pan.at[slot, pl.ds(pl.multiple_of(plane + src * share, 32), share)]

    def sharehalf(slot, h):
        return pan.at[slot, pl.ds(pl.multiple_of(plane + z * share + h * (share // 2), 16), share // 2)]

    def kq(slot, i):
        return kept.at[slot, :, pl.ds(i * q, q)]

    def zpanel(n, slot):
        for step in (1, 3, 2):
            c = pltpu.make_async_remote_copy(
                src_ref=shared(slot, z), dst_ref=shared(slot, z),
                send_sem=psend.at[n, step - 1], recv_sem=psem.at[n, nz - step - 1],
                device_id=(lax.rem(z + step, nz), me), device_id_type=pl.DeviceIdType.MESH,
            )
            c.start()
            pending.append(c)

    def zpanel_wait(n, slot):
        for step in range(1, nz):
            src = lax.rem(z + step, nz)
            pltpu.make_async_remote_copy(
                src_ref=shared(slot, src), dst_ref=shared(slot, src),
                send_sem=psend.at[n, step - 1], recv_sem=psem.at[n, step - 1],
                device_id=(src, me), device_id_type=pl.DeviceIdType.MESH,
            ).wait_recv()

    xq = (0, 1, 2, 3)
    yq = (2, 3, 0, 1)
    send(0, shared(me, z), xn)
    send(1, shared(me, z), yn)
    send(2, inhalf(me, 0), xn)
    send(3, inhalf(me, 1), yn)
    send(13, inhalf(me, 1), xn)
    send(14, inhalf(me, 0), yn)
    send(4, pan.at[me], partner)
    loads[4].wait()
    for l in range(nblocks):
        im = imask_ref[0, 0, l].astype(jnp.float32)
        sl = slice(l * width, (l + 1) * width)
        kept[me, :, :, sl] = (int_ref[:, :, sl].astype(jnp.float32) * im).astype(jnp.bfloat16)
    recv(0, shared(xn, z), xn)
    send(6, sharehalf(xn, 0), yn)
    zpanel(0, xn)
    recv(1, shared(yn, z), yn)
    send(7, sharehalf(yn, 1), xn)
    zpanel(1, yn)
    recv(2, inhalf(xn, 0), xn)
    send(11, inhalf(xn, 0), yn)
    recv(3, inhalf(yn, 1), yn)
    send(12, inhalf(yn, 1), xn)
    for i in range(2):
        send(20 + i, kq(me, xq[i]), xn)
        send(24 + i, kq(me, yq[i]), yn)
    send(5, kept.at[me], partner)
    recv(6, sharehalf(dn, 0), yn)
    recv(7, sharehalf(dn, 1), xn)
    zpanel(2, dn)

    xin = ((xn, 0, 20), (xn, 1, 21), (dn, 2, 28), (xn, 2, 22), (dn, 3, 29), (xn, 3, 23))
    yin = ((yn, 2, 24), (yn, 3, 25), (dn, 0, 30), (yn, 0, 26), (dn, 1, 31), (yn, 1, 27))

    def arrive(t):
        xs, xi, xk = xin[t]
        ys, yi, yk = yin[t]
        recv(xk, kq(xs, xi), xn)
        if t < 2:
            send(30 + t, kq(xs, xi), yn)
            send(26 + t, kq(me, yq[2 + t]), yn)
        send(32 + 2 * t, kq(xs, xi), partner)
        recv(yk, kq(ys, yi), yn)
        if t < 2:
            send(28 + t, kq(ys, yi), xn)
            send(22 + t, kq(me, xq[2 + t]), xn)
        send(33 + 2 * t, kq(ys, yi), partner)

    own = kept[me].reshape(aux_local * rows, nbas)

    def transform(ch, first):
        c = jnp.concatenate([pan[2 * ch], pan[2 * ch + 1]], axis=1)
        half = jnp.dot(own, c, preferred_element_type=jnp.float32).astype(jnp.bfloat16)
        t = lax.dot_general(half, c, NT, preferred_element_type=jnp.float32)
        tacc[...] = t if first else tacc[...] + t

    recv(4, pan.at[partner], partner)
    transform(chip, True)
    recv(13, inhalf(xn, 1), xn)
    zpanel_wait(0, xn)
    send(8, pan.at[xn], partner)
    recv(14, inhalf(yn, 0), yn)
    zpanel_wait(1, yn)
    send(9, pan.at[yn], partner)
    recv(8, pan.at[partner + xn - me], partner)
    transform(xchip, False)
    recv(11, inhalf(dn, 0), yn)
    recv(12, inhalf(dn, 1), xn)
    zpanel_wait(2, dn)
    send(10, pan.at[dn], partner)
    recv(9, pan.at[partner + yn - me], partner)
    transform(ychip, False)
    arrive(0)
    recv(10, pan.at[partner + dn - me], partner)
    transform(dchip, False)
    for p in range(aux_local):
        t = tacc[p * rows:(p + 1) * rows, :]
        hi = t.astype(jnp.bfloat16)
        t2[p, :rows, :] = hi
        t2[p, rows:, :] = (t - hi.astype(jnp.float32)).astype(jnp.bfloat16)

    def zcopy(ch, i):
        slot = lax.rem(z - ch + nz, nz)
        return pltpu.make_async_remote_copy(
            src_ref=part16.at[ch, i], dst_ref=zrecv.at[slot - 1, i],
            send_sem=zsend.at[ch, i], recv_sem=zsem.at[slot - 1, i],
            device_id=(ch, me), device_id_type=pl.DeviceIdType.MESH,
        )

    def product(pieces):
        r = None
        for p in range(aux_local):
            lhs = jnp.concatenate(
                [kept[2 * ch + k, p, i * q:(i + 1) * q, :] for ch, i in pieces for k in range(2)], axis=0
            )
            t = lax.dot_general(lhs, t2[p], NT, preferred_element_type=jnp.float32)
            r = t if r is None else r + t
        r = r[:, :rows] + r[:, rows:]
        for n, (ch, i) in enumerate(pieces):
            part[ch, i] = r[n * 2 * q:(n + 1) * 2 * q]
            part16[ch, i] = r[n * 2 * q:(n + 1) * 2 * q].astype(jnp.bfloat16)
        for ch, i in pieces:
            @pl.when(ch != z)
            def _():
                zcopy(ch, i).start()

    recv(5, kept.at[partner], partner)
    product([(chip, 0), (chip, 1)])
    arrive(1)
    product([(chip, 2), (chip, 3)])
    for t in range(6):
        xs, xi, xk = xin[t]
        ys, yi, yk = yin[t]
        if t >= 2:
            arrive(t)
        recv(32 + 2 * t, kq(partner + xs - me, xi), partner)
        recv(33 + 2 * t, kq(partner + ys - me, yi), partner)
        product([(xs // 2, xi), (ys // 2, yi)])

    for i in range(4):
        total = part[z, i]
        for s in range(nz - 1):
            src = lax.rem(z + s + 1, nz)
            pltpu.make_async_remote_copy(
                src_ref=zrecv.at[s, i], dst_ref=zrecv.at[s, i],
                send_sem=zsend.at[z, i], recv_sem=zsem.at[s, i],
                device_id=(src, me), device_id_type=pl.DeviceIdType.MESH,
            ).wait_recv()
            total += zrecv[s, i].astype(jnp.float32)
        for k in range(2):
            tacc[k * rows + i * q:k * rows + (i + 1) * q, :rows] = total[k * q:(k + 1) * q] * scale
    for k in range(2):
        out_ref[:, k * rows:(k + 1) * rows] = tacc[k * rows:(k + 1) * rows, :rows].T
    for c in pending:
        c.wait_send()
    for step in range(1, nz):
        ch = lax.rem(z + step, nz)
        for i in range(4):
            zcopy(ch, i).wait_send()


def local_kernel(integrals, int_mask, panels, coef_mask, owner_map):
    aux_local, rows, nbas = integrals.shape
    width = panels.shape[1]
    norb, naux = lax.axis_size("orb"), lax.axis_size("aux")
    nocc = width * norb
    scale = float(aux_local * naux * nocc) ** -0.5
    vmem = pl.BlockSpec(memory_space=pltpu.VMEM)
    hbm = pl.BlockSpec(memory_space=pltpu.HBM)
    return pl.pallas_call(
        functools.partial(kernel, scale),
        out_shape=jax.ShapeDtypeStruct((rows, nbas // naux), jnp.float32),
        in_specs=[hbm] * 5,
        out_specs=vmem,
        scratch_shapes=[
            pltpu.VMEM(integrals.shape, jnp.bfloat16),
            pltpu.SMEM(int_mask.shape, jnp.int32),
            pltpu.VMEM(panels.shape, jnp.bfloat16),
            pltpu.SMEM(coef_mask.shape, jnp.int32),
            pltpu.SMEM(owner_map.shape, jnp.int32),
            pltpu.VMEM((norb, nbas, width), jnp.bfloat16),
            pltpu.VMEM((norb, aux_local, rows, nbas), jnp.bfloat16),
            pltpu.VMEM((aux_local * rows, nbas), jnp.float32),
            pltpu.VMEM((aux_local, 2 * rows, nbas), jnp.bfloat16),
            pltpu.VMEM((naux, 4, rows // 2, rows), jnp.float32),
            pltpu.VMEM((naux - 1, 4, rows // 2, rows), jnp.bfloat16),
            pltpu.VMEM((naux, 4, rows // 2, rows), jnp.bfloat16),
            pltpu.SemaphoreType.DMA((5,)),
            pltpu.SemaphoreType.DMA((44,)),
            pltpu.SemaphoreType.DMA((44,)),
            pltpu.SemaphoreType.DMA((naux, 4)),
            pltpu.SemaphoreType.DMA((naux - 1, 4)),
            pltpu.SemaphoreType.DMA((3, naux - 1)),
            pltpu.SemaphoreType.DMA((3, naux - 1)),
        ],
        compiler_params=pltpu.CompilerParams(
            collective_id=0, has_side_effects=True, vmem_limit_bytes=67043328
        ),
    )(integrals, int_mask, panels, coef_mask, owner_map)


def solution(mesh):
    placed = (P("aux", "orb", None), P("aux", "orb", None), P(None, "orb"), P(), P())
    square = mesh.shape["orb"] == 8 and mesh.shape["aux"] == 4
    return jax.shard_map(
        local_kernel if square else local_collectives,
        mesh=mesh, in_specs=placed, out_specs=P("orb", "aux"), check_vma=False,
    )
```

```python
import functools

import jax
import jax.numpy as jnp
from jax import lax
from jax.experimental import pallas as pl
from jax.experimental.pallas import tpu as pltpu
from jax.sharding import PartitionSpec as P

NT = (((1,), (1,)), ((), ()))


def tile_product(mine, other):
    return jnp.einsum("pmi,pni->mn", mine, other, preferred_element_type=jnp.float32)


def local_collectives(integrals, int_mask, panels, coef_mask, owner_map):
    aux_local, rows, nbas = integrals.shape
    nblocks = int_mask.shape[2]
    width = nbas // nblocks
    keep = int_mask[0, 0].astype(jnp.bfloat16)
    kept = (integrals.reshape(aux_local, rows, nblocks, width) * keep[None, None, :, None]).reshape(
        aux_local, rows, nbas
    )
    gathered = lax.all_gather(panels, "orb", axis=1, tiled=True)
    nocc = gathered.shape[1]
    oblocks = nocc // width
    here = (owner_map[:, None] == jnp.arange(oblocks)[None, :]).astype(jnp.bfloat16)
    slot_mask = jnp.dot(coef_mask.astype(jnp.bfloat16), here)
    coef = gathered.reshape(nblocks, width, oblocks, width) * slot_mask[:, None, :, None]
    coef = coef.reshape(nbas, nocc)
    half = jnp.dot(kept.reshape(aux_local * rows, nbas), coef, preferred_element_type=jnp.float32)
    half = half.astype(jnp.bfloat16).reshape(aux_local, rows, nocc)
    partial_rows = tile_product(half, lax.all_gather(half, "orb", axis=1, tiled=True))
    scale_factor = 1.0 / jnp.sqrt(jnp.float32(aux_local * lax.axis_size("aux") * nocc))
    return lax.psum_scatter(partial_rows * scale_factor, "aux", scatter_dimension=1, tiled=True)


def kernel(
    scale, int_hbm, imask_hbm, pan_hbm, cmask_hbm, owner_hbm, out_ref,
    int_ref, imask_ref, pan_ref, cmask_ref, owner_ref,
    pan, kept, tacc, t2, part, zrecv, part16, insem, ssem, rsem, zsend, zsem, psend, psem,
):
    loads = [
        pltpu.make_async_copy(src, dst, insem.at[n])
        for n, (src, dst) in enumerate((
            (imask_hbm, imask_ref), (cmask_hbm, cmask_ref), (owner_hbm, owner_ref),
            (pan_hbm, pan_ref), (int_hbm, int_ref),
        ))
    ]
    for load in loads:
        load.start()
    me = lax.axis_index("orb")
    z = lax.axis_index("aux")
    core = lax.rem(me, 2)
    x = lax.rem(me // 2, 2)
    y = me // 4
    partner = me + 1 - 2 * core
    xn = me + 2 - 4 * x
    yn = me + 4 - 8 * y
    dn = xn + 4 - 8 * y
    chip, xchip, ychip, dchip = me // 2, xn // 2, yn // 2, dn // 2
    nz = 4
    aux_local, rows, nbas = int_ref.shape
    width = pan_ref.shape[1]
    nblocks = nbas // width
    q = rows // 4
    plane = 640
    share = (nbas - plane) // nz

    barrier = pltpu.get_barrier_semaphore()
    for other in (partner, xn, yn):
        pl.semaphore_signal(
            barrier, inc=1, device_id=(z, other), device_id_type=pl.DeviceIdType.MESH
        )
    for step in range(1, nz):
        pl.semaphore_signal(
            barrier, inc=1, device_id=(lax.rem(z + step, nz), me), device_id_type=pl.DeviceIdType.MESH
        )
    for load in loads[:4]:
        load.wait()

    block = jnp.int32(0)
    for j in range(nblocks):
        block = jnp.where(owner_ref[j] == me, j, block)
    for l in range(nblocks):
        cm = cmask_ref[l, block].astype(jnp.float32)
        sl = slice(l * width, (l + 1) * width)
        pan[me, sl, :] = (pan_ref[sl, :].astype(jnp.float32) * cm).astype(jnp.bfloat16)

    pl.semaphore_wait(barrier, 3 + nz - 1)

    pending = []

    def copy(kind, ref, dev):
        return pltpu.make_async_remote_copy(
            src_ref=ref, dst_ref=ref, send_sem=ssem.at[kind], recv_sem=rsem.at[kind],
            device_id=(z, dev), device_id_type=pl.DeviceIdType.MESH,
        )

    def send(kind, ref, dev):
        c = copy(kind, ref, dev)
        c.start()
        pending.append(c)

    def recv(kind, ref, dev):
        copy(kind, ref, dev).wait_recv()

    def inhalf(slot, h):
        return pan.at[slot, pl.ds(h * plane // 2, plane // 2)]

    def shared(slot, src):
        return pan.at[slot, pl.ds(pl.multiple_of(plane + src * share, 32), share)]

    def sharehalf(slot, h):
        return pan.at[slot, pl.ds(pl.multiple_of(plane + z * share + h * (share // 2), 16), share // 2)]

    def kq(slot, i):
        return kept.at[slot, :, pl.ds(i * q, q)]

    def zpanel(n, slot):
        for step in (1, 3, 2):
            c = pltpu.make_async_remote_copy(
                src_ref=shared(slot, z), dst_ref=shared(slot, z),
                send_sem=psend.at[n, step - 1], recv_sem=psem.at[n, nz - step - 1],
                device_id=(lax.rem(z + step, nz), me), device_id_type=pl.DeviceIdType.MESH,
            )
            c.start()
            pending.append(c)

    def zpanel_wait(n, slot):
        for step in range(1, nz):
            src = lax.rem(z + step, nz)
            pltpu.make_async_remote_copy(
                src_ref=shared(slot, src), dst_ref=shared(slot, src),
                send_sem=psend.at[n, step - 1], recv_sem=psem.at[n, step - 1],
                device_id=(src, me), device_id_type=pl.DeviceIdType.MESH,
            ).wait_recv()

    xq = (0, 1, 2, 3)
    yq = (2, 3, 0, 1)
    send(0, shared(me, z), xn)
    send(1, shared(me, z), yn)
    send(2, inhalf(me, 0), xn)
    send(3, inhalf(me, 1), yn)
    send(13, inhalf(me, 1), xn)
    send(14, inhalf(me, 0), yn)
    send(4, pan.at[me], partner)
    loads[4].wait()
    for l in range(nblocks):
        im = imask_ref[0, 0, l].astype(jnp.float32)
        sl = slice(l * width, (l + 1) * width)
        kept[me, :, :, sl] = (int_ref[:, :, sl].astype(jnp.float32) * im).astype(jnp.bfloat16)
    recv(0, shared(xn, z), xn)
    send(6, sharehalf(xn, 0), yn)
    zpanel(0, xn)
    recv(1, shared(yn, z), yn)
    send(7, sharehalf(yn, 1), xn)
    zpanel(1, yn)
    recv(2, inhalf(xn, 0), xn)
    send(11, inhalf(xn, 0), yn)
    recv(3, inhalf(yn, 1), yn)
    send(12, inhalf(yn, 1), xn)
    for i in range(2):
        send(20 + i, kq(me, xq[i]), xn)
        send(24 + i, kq(me, yq[i]), yn)
    send(5, kept.at[me], partner)
    recv(6, sharehalf(dn, 0), yn)
    recv(7, sharehalf(dn, 1), xn)
    zpanel(2, dn)

    xin = ((xn, 0, 20), (xn, 1, 21), (dn, 2, 28), (xn, 2, 22), (dn, 3, 29), (xn, 3, 23))
    yin = ((yn, 2, 24), (yn, 3, 25), (dn, 0, 30), (yn, 0, 26), (dn, 1, 31), (yn, 1, 27))

    def arrive(t):
        xs, xi, xk = xin[t]
        ys, yi, yk = yin[t]
        recv(xk, kq(xs, xi), xn)
        if t < 2:
            send(30 + t, kq(xs, xi), yn)
            send(26 + t, kq(me, yq[2 + t]), yn)
        send(32 + 2 * t, kq(xs, xi), partner)
        recv(yk, kq(ys, yi), yn)
        if t < 2:
            send(28 + t, kq(ys, yi), xn)
            send(22 + t, kq(me, xq[2 + t]), xn)
        send(33 + 2 * t, kq(ys, yi), partner)

    own = kept[me].reshape(aux_local * rows, nbas)

    def transform(ch, first):
        c = jnp.concatenate([pan[2 * ch], pan[2 * ch + 1]], axis=1)
        half = jnp.dot(own, c, preferred_element_type=jnp.float32).astype(jnp.bfloat16)
        t = lax.dot_general(half, c, NT, preferred_element_type=jnp.float32)
        tacc[...] = t if first else tacc[...] + t

    recv(4, pan.at[partner], partner)
    transform(chip, True)
    recv(13, inhalf(xn, 1), xn)
    zpanel_wait(0, xn)
    send(8, pan.at[xn], partner)
    recv(14, inhalf(yn, 0), yn)
    zpanel_wait(1, yn)
    send(9, pan.at[yn], partner)
    recv(8, pan.at[partner + xn - me], partner)
    transform(xchip, False)
    recv(11, inhalf(dn, 0), yn)
    recv(12, inhalf(dn, 1), xn)
    zpanel_wait(2, dn)
    send(10, pan.at[dn], partner)
    recv(9, pan.at[partner + yn - me], partner)
    transform(ychip, False)
    arrive(0)
    recv(10, pan.at[partner + dn - me], partner)
    transform(dchip, False)
    for p in range(aux_local):
        t = tacc[p * rows:(p + 1) * rows, :]
        hi = t.astype(jnp.bfloat16)
        t2[p, :rows, :] = hi
        t2[p, rows:, :] = (t - hi.astype(jnp.float32)).astype(jnp.bfloat16)

    def zcopy(ch, i):
        slot = lax.rem(z - ch + nz, nz)
        return pltpu.make_async_remote_copy(
            src_ref=part16.at[ch, i], dst_ref=zrecv.at[slot - 1, i],
            send_sem=zsend.at[ch, i], recv_sem=zsem.at[slot - 1, i],
            device_id=(ch, me), device_id_type=pl.DeviceIdType.MESH,
        )

    def product(pieces):
        r = None
        for p in range(aux_local):
            lhs = jnp.concatenate(
                [kept[2 * ch + k, p, i * q:(i + 1) * q, :] for ch, i in pieces for k in range(2)], axis=0
            )
            t = lax.dot_general(lhs, t2[p], NT, preferred_element_type=jnp.float32)
            r = t if r is None else r + t
        r = r[:, :rows] + r[:, rows:]
        for n, (ch, i) in enumerate(pieces):
            part[ch, i] = r[n * 2 * q:(n + 1) * 2 * q]
            part16[ch, i] = r[n * 2 * q:(n + 1) * 2 * q].astype(jnp.bfloat16)
        for ch, i in pieces:
            @pl.when(ch != z)
            def _():
                zcopy(ch, i).start()

    recv(5, kept.at[partner], partner)
    product([(chip, 0), (chip, 1)])
    arrive(1)
    product([(chip, 2), (chip, 3)])
    for t in range(6):
        xs, xi, xk = xin[t]
        ys, yi, yk = yin[t]
        if t >= 2:
            arrive(t)
        recv(32 + 2 * t, kq(partner + xs - me, xi), partner)
        recv(33 + 2 * t, kq(partner + ys - me, yi), partner)
        product([(xs // 2, xi), (ys // 2, yi)])

    for i in range(4):
        total = part[z, i]
        for s in range(nz - 1):
            src = lax.rem(z + s + 1, nz)
            pltpu.make_async_remote_copy(
                src_ref=zrecv.at[s, i], dst_ref=zrecv.at[s, i],
                send_sem=zsend.at[z, i], recv_sem=zsem.at[s, i],
                device_id=(src, me), device_id_type=pl.DeviceIdType.MESH,
            ).wait_recv()
            total += zrecv[s, i].astype(jnp.float32)
        for k in range(2):
            tacc[k * rows + i * q:k * rows + (i + 1) * q, :rows] = total[k * q:(k + 1) * q] * scale
    for k in range(2):
        out_ref[:, k * rows:(k + 1) * rows] = tacc[k * rows:(k + 1) * rows, :rows].T
    for c in pending:
        c.wait_send()
    for step in range(1, nz):
        ch = lax.rem(z + step, nz)
        for i in range(4):
            zcopy(ch, i).wait_send()


def local_kernel(integrals, int_mask, panels, coef_mask, owner_map):
    aux_local, rows, nbas = integrals.shape
    width = panels.shape[1]
    norb, naux = lax.axis_size("orb"), lax.axis_size("aux")
    nocc = width * norb
    scale = float(aux_local * naux * nocc) ** -0.5
    vmem = pl.BlockSpec(memory_space=pltpu.VMEM)
    hbm = pl.BlockSpec(memory_space=pltpu.HBM)
    operands = [
        pltpu.with_memory_space_constraint(a, pltpu.HBM)
        for a in (integrals, int_mask, panels, coef_mask, owner_map)
    ]
    return pl.pallas_call(
        functools.partial(kernel, scale),
        out_shape=pltpu.VMEM((rows, nbas // naux), jnp.float32),
        in_specs=[hbm] * 5,
        out_specs=vmem,
        scratch_shapes=[
            pltpu.VMEM(integrals.shape, jnp.bfloat16),
            pltpu.SMEM(int_mask.shape, jnp.int32),
            pltpu.VMEM(panels.shape, jnp.bfloat16),
            pltpu.SMEM(coef_mask.shape, jnp.int32),
            pltpu.SMEM(owner_map.shape, jnp.int32),
            pltpu.VMEM((norb, nbas, width), jnp.bfloat16),
            pltpu.VMEM((norb, aux_local, rows, nbas), jnp.bfloat16),
            pltpu.VMEM((aux_local * rows, nbas), jnp.float32),
            pltpu.VMEM((aux_local, 2 * rows, nbas), jnp.bfloat16),
            pltpu.VMEM((naux, 4, rows // 2, rows), jnp.float32),
            pltpu.VMEM((naux - 1, 4, rows // 2, rows), jnp.bfloat16),
            pltpu.VMEM((naux, 4, rows // 2, rows), jnp.bfloat16),
            pltpu.SemaphoreType.DMA((5,)),
            pltpu.SemaphoreType.DMA((44,)),
            pltpu.SemaphoreType.DMA((44,)),
            pltpu.SemaphoreType.DMA((naux, 4)),
            pltpu.SemaphoreType.DMA((naux - 1, 4)),
            pltpu.SemaphoreType.DMA((3, naux - 1)),
            pltpu.SemaphoreType.DMA((3, naux - 1)),
        ],
        compiler_params=pltpu.CompilerParams(
            collective_id=0, has_side_effects=True, vmem_limit_bytes=33554432
        ),
    )(*operands)


def solution(mesh):
    placed = (P("aux", "orb", None), P("aux", "orb", None), P(None, "orb"), P(), P())
    square = mesh.shape["orb"] == 8 and mesh.shape["aux"] == 4
    return jax.shard_map(
        local_kernel if square else local_collectives,
        mesh=mesh, in_specs=placed, out_specs=P("orb", "aux"), check_vma=False,
    )
```

```python
import functools

import jax
import jax.numpy as jnp
from jax import lax
from jax.experimental import pallas as pl
from jax.experimental.pallas import tpu as pltpu
from jax.sharding import PartitionSpec as P

NT = (((1,), (1,)), ((), ()))


def tile_product(mine, other):
    return jnp.einsum("pmi,pni->mn", mine, other, preferred_element_type=jnp.float32)


def local_collectives(integrals, int_mask, panels, coef_mask, owner_map):
    aux_local, rows, nbas = integrals.shape
    nblocks = int_mask.shape[2]
    width = nbas // nblocks
    keep = int_mask[0, 0].astype(jnp.bfloat16)
    kept = (integrals.reshape(aux_local, rows, nblocks, width) * keep[None, None, :, None]).reshape(
        aux_local, rows, nbas
    )
    gathered = lax.all_gather(panels, "orb", axis=1, tiled=True)
    nocc = gathered.shape[1]
    oblocks = nocc // width
    here = (owner_map[:, None] == jnp.arange(oblocks)[None, :]).astype(jnp.bfloat16)
    slot_mask = jnp.dot(coef_mask.astype(jnp.bfloat16), here)
    coef = gathered.reshape(nblocks, width, oblocks, width) * slot_mask[:, None, :, None]
    coef = coef.reshape(nbas, nocc)
    half = jnp.dot(kept.reshape(aux_local * rows, nbas), coef, preferred_element_type=jnp.float32)
    half = half.astype(jnp.bfloat16).reshape(aux_local, rows, nocc)
    partial_rows = tile_product(half, lax.all_gather(half, "orb", axis=1, tiled=True))
    scale_factor = 1.0 / jnp.sqrt(jnp.float32(aux_local * lax.axis_size("aux") * nocc))
    return lax.psum_scatter(partial_rows * scale_factor, "aux", scatter_dimension=1, tiled=True)


def kernel(
    scale, int_hbm, imask_hbm, pan_hbm, cmask_hbm, owner_hbm, out_ref,
    int_ref, imask_ref, pan_ref, cmask_ref, owner_ref,
    pan, kept, tacc, t2, part, part16, zrecv, zdiag, msend, mrecv, total,
    insem, ssem, rsem, psend, psem, zsend, zsem, zdsem,
):
    loads = [
        pltpu.make_async_copy(src, dst, insem.at[n])
        for n, (src, dst) in enumerate((
            (imask_hbm, imask_ref), (cmask_hbm, cmask_ref), (owner_hbm, owner_ref),
            (pan_hbm, pan_ref), (int_hbm, int_ref),
        ))
    ]
    for load in loads:
        load.start()
    me = lax.axis_index("orb")
    z = lax.axis_index("aux")
    core = lax.rem(me, 2)
    x = lax.rem(me // 2, 2)
    y = me // 4
    partner = me + 1 - 2 * core
    xn = me + 2 - 4 * x
    yn = me + 4 - 8 * y
    dn = xn + 4 - 8 * y
    chip, xchip, ychip, dchip = me // 2, xn // 2, yn // 2, dn // 2
    py = lax.rem(x + y, 2)
    px = 1 - py
    nz = 4
    aux_local, rows, nbas = int_ref.shape
    width = pan_ref.shape[1]
    nblocks = nbas // width
    npiece = 4
    q = rows // npiece
    hq = rows // 2
    plane = 640
    share = (nbas - plane) // nz

    barrier = pltpu.get_barrier_semaphore()
    greeted = (partner, xn, yn, xn + 1 - 2 * core, yn + 1 - 2 * core)
    for other in greeted:
        pl.semaphore_signal(
            barrier, inc=1, device_id=(z, other), device_id_type=pl.DeviceIdType.MESH
        )
    for step in range(1, nz):
        pl.semaphore_signal(
            barrier, inc=1, device_id=(lax.rem(z + step, nz), me), device_id_type=pl.DeviceIdType.MESH
        )
    for load in loads[:4]:
        load.wait()

    block = jnp.int32(0)
    for j in range(nblocks):
        block = jnp.where(owner_ref[j] == me, j, block)
    for l in range(nblocks):
        cm = cmask_ref[l, block].astype(jnp.float32)
        sl = slice(l * width, (l + 1) * width)
        pan[me, sl, :] = (pan_ref[sl, :].astype(jnp.float32) * cm).astype(jnp.bfloat16)
    loads[4].wait()
    for l in range(nblocks):
        im = imask_ref[0, 0, l].astype(jnp.float32)
        sl = slice(l * width, (l + 1) * width)
        kept[me, :, :, sl] = (int_ref[:, :, sl].astype(jnp.float32) * im).astype(jnp.bfloat16)

    pl.semaphore_wait(barrier, len(greeted) + nz - 1)

    pending = []
    kinds = {}

    def copy(kind, src, dst, dev):
        n = kinds.setdefault(kind, len(kinds))
        return pltpu.make_async_remote_copy(
            src_ref=src, dst_ref=dst, send_sem=ssem.at[n], recv_sem=rsem.at[n],
            device_id=(z, dev), device_id_type=pl.DeviceIdType.MESH,
        )

    def send(kind, ref, dev, dst=None):
        c = copy(kind, ref, ref if dst is None else dst, dev)
        c.start()
        pending.append(c)

    def recv(kind, ref, dev):
        copy(kind, ref, ref, dev).wait_recv()

    def inhalf(slot, h):
        return pan.at[slot, pl.ds(h * plane // 2, plane // 2)]

    def shared(slot, src):
        return pan.at[slot, pl.ds(pl.multiple_of(plane + src * share, 32), share)]

    def sharehalf(slot, h):
        return pan.at[slot, pl.ds(pl.multiple_of(plane + z * share + h * (share // 2), 16), share // 2)]

    def kp(slot, p, i):
        return kept.at[slot, p, pl.ds(i * q, q)]

    def zpanel(n, slot):
        for step in (1, 3, 2):
            c = pltpu.make_async_remote_copy(
                src_ref=shared(slot, z), dst_ref=shared(slot, z),
                send_sem=psend.at[n, step - 1], recv_sem=psem.at[n, nz - step - 1],
                device_id=(lax.rem(z + step, nz), me), device_id_type=pl.DeviceIdType.MESH,
            )
            c.start()
            pending.append(c)

    def zpanel_wait(n, slot):
        for step in range(1, nz):
            src = lax.rem(z + step, nz)
            pltpu.make_async_remote_copy(
                src_ref=shared(slot, src), dst_ref=shared(slot, src),
                send_sem=psend.at[n, step - 1], recv_sem=psem.at[n, step - 1],
                device_id=(src, me), device_id_type=pl.DeviceIdType.MESH,
            ).wait_recv()

    def ksend(i):
        send(("x", i), kp(me, py, i), xn)
        send(("y", i), kp(me, px, i), yn)

    def arrive(t):
        xs, ys, i = (xn, yn, t) if t < npiece else (dn, dn, t - npiece)
        recv(("x", t), kp(xs, px, i), xn)
        if t < npiece:
            send(("y", t + npiece), kp(xs, px, i), yn)
        send(("px", t), kp(xs, px, i), partner)
        recv(("y", t), kp(ys, py, i), yn)
        if t < npiece:
            send(("x", t + npiece), kp(ys, py, i), xn)
        send(("py", t), kp(ys, py, i), partner)
        if t + 4 < npiece:
            ksend(t + 4)

    def relayed(t):
        xs, ys, i = (xn, yn, t) if t < npiece else (dn, dn, t - npiece)
        recv(("px", t), kp(partner + xs - me, px, i), partner)
        recv(("py", t), kp(partner + ys - me, py, i), partner)

    own = kept[me].reshape(aux_local * rows, nbas)

    def transform(ch, first):
        c = jnp.concatenate([pan[2 * ch], pan[2 * ch + 1]], axis=1)
        half = jnp.dot(own, c, preferred_element_type=jnp.float32).astype(jnp.bfloat16)
        t = lax.dot_general(half, c, NT, preferred_element_type=jnp.float32)
        tacc[...] = t if first else tacc[...] + t

    def direct(slot):
        return pan.at[slot, pl.ds(0, plane)]

    def rest(slot):
        return pan.at[slot, pl.ds(plane, nbas - plane)]

    def relay(name, part_of, slot):
        send(name, part_of(slot), partner)

    def relay_wait(name, part_of, slot):
        recv(name, part_of(partner + slot - me), partner)

    send("xs", shared(me, z), xn)
    send("ys", shared(me, z), yn)
    send("x0", inhalf(me, 0), xn)
    send("y1", inhalf(me, 1), yn)
    send("own", pan.at[me], partner)
    send("kown", kept.at[me], partner)
    recv("xs", shared(xn, z), xn)
    send("yfs", sharehalf(xn, 0), yn)
    zpanel(0, xn)
    recv("ys", shared(yn, z), yn)
    send("xfs", sharehalf(yn, 1), xn)
    zpanel(1, yn)
    send("x1", inhalf(me, 1), xn)
    send("y0", inhalf(me, 0), yn)
    recv("own", pan.at[partner], partner)
    transform(chip, True)
    recv("x0", inhalf(xn, 0), xn)
    send("yf0", inhalf(xn, 0), yn)
    recv("y1", inhalf(yn, 1), yn)
    send("xf1", inhalf(yn, 1), xn)
    for i in range(4):
        ksend(i)
    recv("yfs", sharehalf(dn, 0), yn)
    recv("xfs", sharehalf(dn, 1), xn)
    zpanel(2, dn)
    recv("x1", inhalf(xn, 1), xn)
    relay("dx", direct, xn)
    recv("y0", inhalf(yn, 0), yn)
    relay("dy", direct, yn)
    recv("yf0", inhalf(dn, 0), yn)
    recv("xf1", inhalf(dn, 1), xn)
    relay("dd", direct, dn)
    arrive(0)
    zpanel_wait(0, xn)
    relay("rx", rest, xn)
    zpanel_wait(1, yn)
    relay("ry", rest, yn)
    relay_wait("dx", direct, xn)
    relay_wait("rx", rest, xn)
    transform(xchip, False)
    arrive(1)
    relay_wait("dy", direct, yn)
    relay_wait("ry", rest, yn)
    transform(ychip, False)
    zpanel_wait(2, dn)
    relay("rd", rest, dn)
    arrive(2)
    relay_wait("dd", direct, dn)
    relay_wait("rd", rest, dn)
    transform(dchip, False)
    for p in range(aux_local):
        t = tacc[p * rows:(p + 1) * rows, :]
        hi = t.astype(jnp.bfloat16)
        t2[p, :rows, :] = hi
        t2[p, rows:, :] = (t - hi.astype(jnp.float32)).astype(jnp.bfloat16)
    arrive(3)

    def product(ch, fns, lo, n):
        r = None
        for p in fns:
            lhs = jnp.concatenate([kept[2 * ch + k, p, lo:lo + n, :] for k in range(2)], axis=0)
            t = lax.dot_general(lhs, t2[p], NT, preferred_element_type=jnp.float32)
            r = t if r is None else r + t
        return r[:, :rows] + r[:, rows:]

    def zcopy(ch, h):
        slot = lax.rem(z - ch + nz, nz)
        if h is None:
            src, dst, sem, n = part.at[0], zdiag.at[slot - 1], zdsem.at[slot - 1], 0
        elif h < 0:
            src, dst, sem, n = part16.at[ch], zrecv.at[slot - 1], zsem.at[slot - 1], -h
        else:
            src, dst, sem, n = part16.at[ch, h], zrecv.at[slot - 1, h], zsem.at[slot - 1], 3 + h
        return pltpu.make_async_remote_copy(
            src_ref=src, dst_ref=dst, send_sem=zsend.at[n], recv_sem=sem,
            device_id=(ch, me), device_id_type=pl.DeviceIdType.MESH,
        )

    zsent = []

    def zstart(ch, h):
        @pl.when(ch != z)
        def _():
            zcopy(ch, h).start()
        zsent.append((ch, h))

    recv("kown", kept.at[partner], partner)
    part[0] = product(chip, (0, 1), 0, rows)
    zstart(chip, None)

    def mirror(j, ch, dev, p, name):
        for t in range(npiece):
            i = t
            recv((name, t), kp(partner + dev - me, p, i), partner)
        r = product(ch, (p,), 0, rows)
        part[1 + j] = r
        m = r.T.astype(jnp.bfloat16)
        for k in range(2):
            msend[j, k] = m[:, k * rows:(k + 1) * rows]
        for same in range(2):
            other = dev if same else dev + 1 - 2 * core
            k = core if same else 1 - core
            send(("m", j, same), msend.at[j, k], other, dst=mrecv.at[j, core])

    def merge(j, ch, dev):
        for same in range(2):
            k = core if same else 1 - core
            other = dev if same else dev + 1 - 2 * core
            copy(("m", j, same), msend.at[j, k], mrecv.at[j, k], other).wait_recv()
        for k in range(2):
            r = part[1 + j, k * rows:(k + 1) * rows] + mrecv[j, k].astype(jnp.float32)
            part[1 + j, k * rows:(k + 1) * rows] = r
            for h in range(2):
                part16[ch, h, k] = r[h * hq:(h + 1) * hq].astype(jnp.bfloat16)
        zstart(ch, -1 - j)

    mirror(0, xchip, xn, px, "px")
    mirror(1, ychip, yn, py, "py")

    def across(h):
        r = product(dchip, (0, 1), h * hq, hq)
        for k in range(2):
            part[3, k * rows + h * hq:k * rows + (h + 1) * hq] = r[k * hq:(k + 1) * hq]
            part16[dchip, h, k] = r[k * hq:(k + 1) * hq].astype(jnp.bfloat16)
        zstart(dchip, h)

    arrive(4)
    arrive(5)
    merge(0, xchip, xn)
    merge(1, ychip, yn)
    relayed(4)
    relayed(5)
    across(0)
    arrive(6)
    arrive(7)
    relayed(6)
    relayed(7)
    across(1)

    @pl.when(z == chip)
    def _():
        t = part[0]
        for s in range(nz - 1):
            zwait(zdiag.at[s], zdsem.at[s], zsend.at[0], z, me)
            t += zdiag[s]
        total[...] = t

    @pl.when(z != chip)
    def _():
        mine = jnp.where(z == xchip, 1, jnp.where(z == ychip, 2, 3))
        t = part[mine]
        for s in range(nz - 1):
            zwait(zrecv.at[s], zsem.at[s], zsend.at[0], z, me)
            t += jnp.concatenate(
                [zrecv[s, h, k] for k in range(2) for h in range(2)], axis=0
            ).astype(jnp.float32)
        total[...] = t

    for k in range(2):
        out_ref[:, k * rows:(k + 1) * rows] = (total[k * rows:(k + 1) * rows, :] * scale).T
    for c in pending:
        c.wait_send()
    for ch, h in zsent:
        @pl.when(ch != z)
        def _():
            zcopy(ch, h).wait_send()


def zwait(ref, recv_sem, send_sem, z, me):
    pltpu.make_async_remote_copy(
        src_ref=ref, dst_ref=ref, send_sem=send_sem, recv_sem=recv_sem,
        device_id=(lax.rem(z + 1, 4), me), device_id_type=pl.DeviceIdType.MESH,
    ).wait_recv()


def local_kernel(integrals, int_mask, panels, coef_mask, owner_map):
    aux_local, rows, nbas = integrals.shape
    width = panels.shape[1]
    norb, naux = lax.axis_size("orb"), lax.axis_size("aux")
    nocc = width * norb
    scale = float(aux_local * naux * nocc) ** -0.5
    vmem = pl.BlockSpec(memory_space=pltpu.VMEM)
    hbm = pl.BlockSpec(memory_space=pltpu.HBM)
    operands = [
        pltpu.with_memory_space_constraint(a, pltpu.HBM)
        for a in (integrals, int_mask, panels, coef_mask, owner_map)
    ]
    return pl.pallas_call(
        functools.partial(kernel, scale),
        out_shape=pltpu.VMEM((rows, nbas // naux), jnp.float32),
        in_specs=[hbm] * 5,
        out_specs=vmem,
        scratch_shapes=[
            pltpu.VMEM(integrals.shape, jnp.bfloat16),
            pltpu.SMEM(int_mask.shape, jnp.int32),
            pltpu.VMEM(panels.shape, jnp.bfloat16),
            pltpu.SMEM(coef_mask.shape, jnp.int32),
            pltpu.SMEM(owner_map.shape, jnp.int32),
            pltpu.VMEM((norb, nbas, width), jnp.bfloat16),
            pltpu.VMEM((norb, aux_local, rows, nbas), jnp.bfloat16),
            pltpu.VMEM((aux_local * rows, nbas), jnp.float32),
            pltpu.VMEM((aux_local, 2 * rows, nbas), jnp.bfloat16),
            pltpu.VMEM((4, 2 * rows, rows), jnp.float32),
            pltpu.VMEM((naux, 2, 2, rows // 2, rows), jnp.bfloat16),
            pltpu.VMEM((naux - 1, 2, 2, rows // 2, rows), jnp.bfloat16),
            pltpu.VMEM((naux - 1, 2 * rows, rows), jnp.float32),
            pltpu.VMEM((2, 2, rows, rows), jnp.bfloat16),
            pltpu.VMEM((2, 2, rows, rows), jnp.bfloat16),
            pltpu.VMEM((2 * rows, rows), jnp.float32),
            pltpu.SemaphoreType.DMA((5,)),
            pltpu.SemaphoreType.DMA((64,)),
            pltpu.SemaphoreType.DMA((64,)),
            pltpu.SemaphoreType.DMA((3, naux - 1)),
            pltpu.SemaphoreType.DMA((3, naux - 1)),
            pltpu.SemaphoreType.DMA((5,)),
            pltpu.SemaphoreType.DMA((naux - 1,)),
            pltpu.SemaphoreType.DMA((naux - 1,)),
        ],
        compiler_params=pltpu.CompilerParams(
            collective_id=0, has_side_effects=True, vmem_limit_bytes=33554432
        ),
    )(*operands)


def solution(mesh):
    placed = (P("aux", "orb", None), P("aux", "orb", None), P(None, "orb"), P(), P())
    square = mesh.shape["orb"] == 8 and mesh.shape["aux"] == 4
    return jax.shard_map(
        local_kernel if square else local_collectives,
        mesh=mesh, in_specs=placed, out_specs=P("orb", "aux"), check_vma=False,
    )
```
